512 devices in a mesh: dof: 64 (over z, y_lo, core), real: 8 (over y_hi, x).
Axes of the slice: x: 4, y: 8 (y_hi: 2, y_lo: 4; y = y_hi * 4 + y_lo), z: 8, core: 2. Of those that a mesh axis runs over, the one named last changes fastest.
Arguments:
- mode_panel: bfloat16 [131072, 512], P('dof'), may hold values from -0.31445312 to 0.31445312
- stiff_blocks: bfloat16 [1024, 5, 128, 128], P('dof'), as said below
- stiff_cols: int32 [1024, 5], P('dof'), may hold values from 0 to 1023, as said below
- row_blade: int32 [131072], P('dof'), may hold values from 0 to 3, as said below
- adjusted_values: float32 [512], replicated, may hold values from 4 to 24
- deviations: float32 [128, 4], P('dof'), may hold values from -0.05 to 0.05
- start_block: float32 [512, 128], P('real'), may hold values from -6 to 6
Outputs:
- projected: float32 [4, 512, 512], P(None, 'real')
- subspace: float32 [128, 512, 128], P('dof', 'real')
The draws below stay inside these ranges and needn't reach their ends.
Inputs may be any that keep to these rules, and one draw needn't show every extreme that they name: `stiff_cols`: each block row's 5 entries are, in some order, the block row itself and the block rows two and one before and one and two after it; where one of those lies outside the grid or in another blade's rows, the block row itself stands in. `stiff_blocks`: the stiffness is symmetric and couples no two blades: the block of block row g at column c is the transpose of the block of block row c at column g, diagonal blocks are symmetric, and stand-in blocks are zero. `row_blade`: block row g belongs to the blade numbered ((g + 8) // 256) mod 4 under a fixed relabelling of the blades; so each blade owns a run of 32768 neighbouring rows, except one blade, which owns the first 31744 rows and the last 1024 rows.
All inputs are finite; a program needn't handle non-finite values.
Results may differ from the reference program's by a relative error of at most 0.003.
Values may be sent and summed in bfloat16 or wider, within the bound.
No kernel may reach another device: no remote copies, remote signals or barrier semaphores. Data moves between devices by JAX's collectives and lax.ppermute only.
A program may use at most 64 MiB of HBM per device.

```python
import jax
import jax.numpy as jnp
from jax import lax

ADJUSTED_MODES = 512
S = 128
BS = 128
NBR = 5
NBLADE = 4
STEPS = 2
SHARD_BLOCKS = 16
NB = 1024
NROWS = 131072
REALS = 128


def blade_of_block(block_rows):
    run_length = NB // NBLADE
    return (block_rows + SHARD_BLOCKS // 2) // run_length % NBLADE


def coupling_pattern(key):
    block_rows = jnp.arange(NB, dtype=jnp.int32)
    base_offsets = jnp.array([0, -2, -1, 1, 2], dtype=jnp.int32)
    row_keys = jax.random.split(jax.random.fold_in(key, 7), NB)
    sort_indices = jax.vmap(lambda one_key: jax.random.permutation(one_key, 5))(row_keys).astype(jnp.int32)
    offsets = base_offsets[sort_indices]
    target = block_rows[:, None] + offsets
    inside = (target >= 0) & (target < NB) & (blade_of_block(target) == blade_of_block(block_rows)[:, None])
    columns = jnp.where(inside, target, block_rows[:, None])
    return (sort_indices, inside, columns)


def draw_stiff_cols(key, part):
    sort_indices, inside, columns = coupling_pattern(key)
    return columns.astype(jnp.int32)


def draw_stiff_blocks(key, part):
    sort_indices, inside, columns = coupling_pattern(key)
    scale = (5.0 * BS) ** (-0.5)
    upper_one = jax.random.normal(jax.random.fold_in(key, 1), (NB, BS, BS), jnp.float32) * scale
    upper_two = jax.random.normal(jax.random.fold_in(key, 2), (NB, BS, BS), jnp.float32) * scale
    raw_diag = jax.random.normal(jax.random.fold_in(key, 3), (NB, BS, BS), jnp.float32) * scale
    diag_sym = (raw_diag + jnp.swapaxes(raw_diag, 1, 2)) * 0.5 ** 0.5
    lower_two = jnp.swapaxes(jnp.roll(upper_two, 2, axis=0), 1, 2)
    lower_one = jnp.swapaxes(jnp.roll(upper_one, 1, axis=0), 1, 2)
    candidates = jnp.stack([diag_sym, lower_two, lower_one, upper_one, upper_two], axis=1)
    picked = jnp.take_along_axis(candidates, sort_indices[:, :, None, None], axis=1)
    picked = jnp.where(inside[:, :, None, None], picked, jnp.zeros_like(picked))
    return picked.astype(jnp.bfloat16)


def draw_row_blade(key, part):
    labels = jax.random.permutation(key, NBLADE).astype(jnp.int32)
    block_index = jnp.arange(NROWS, dtype=jnp.int32) // BS
    return labels[blade_of_block(block_index)]


def draw_adjusted_values(key, part):
    position = jnp.arange(ADJUSTED_MODES, dtype=jnp.float32)
    trend = 4.0 * jnp.exp(jnp.log(3.0) * position / (ADJUSTED_MODES - 1))
    spread = jax.random.uniform(key, (ADJUSTED_MODES,), jnp.float32)
    return trend * jnp.exp(jnp.log(2.0) * spread)


def shard_levels(key, dims, cuts, least, top_value):
    gain = 1.0
    for dim, shards_of in cuts:
        steps = jax.random.uniform(jax.random.fold_in(jax.random.fold_in(key, 6), dim), (shards_of,), jnp.float32, least / len(cuts), top_value / len(cuts))
        gain = gain * jnp.repeat(jnp.exp(steps), dims[dim] // shards_of).reshape((-1,) + (1,) * (len(dims) - 1 - dim))
    return gain


def normal_values(stream_key, dims, deviation, most, cuts=(), kind=jnp.bfloat16):
    values = deviation * jax.random.normal(stream_key, dims, jnp.float32)
    if cuts:
        values = values * shard_levels(stream_key, dims, cuts, -0.22, 0.18)
    return jnp.clip(values, -most, most).astype(kind)


def setup_inputs(seed: int = 0) -> dict:
    keys = jax.random.split(jax.random.key(seed), 8)
    return {
        "mode_panel": normal_values(keys[0], (NROWS, ADJUSTED_MODES), (NROWS ** -0.25), 0.31445312, ((0, 64),)),
        "stiff_blocks": draw_stiff_blocks(jax.random.fold_in(keys[7], 71), 0),
        "stiff_cols": draw_stiff_cols(jax.random.fold_in(keys[7], 71), 0),
        "row_blade": draw_row_blade(jax.random.fold_in(keys[7], 71), 0),
        "adjusted_values": draw_adjusted_values(jax.random.fold_in(keys[7], 71), 0),
        "deviations": jnp.clip(jax.random.uniform(keys[5], (REALS, NBLADE), jnp.float32, -0.05, 0.05) * shard_levels(keys[5], (REALS, NBLADE), ((0, 64),), -0.4, 0.0), -0.05, 0.05),
        "start_block": normal_values(keys[6], (ADJUSTED_MODES, S), 1.0, 6.0, ((0, 8),), jnp.float32),
    }


highest_accuracy = lax.Precision.HIGHEST

def stiffness_image(mode_panel, stiff_blocks, stiff_cols):
    number = stiff_blocks.shape[0]
    blocks = mode_panel.reshape(number, BS, ADJUSTED_MODES).astype(jnp.float32)
    row_totals = jnp.zeros((number, BS, ADJUSTED_MODES), jnp.float32)
    for slot_index in range(NBR):
        picked = jnp.take(blocks, stiff_cols[:, slot_index], axis=0)
        row_totals = row_totals + jnp.einsum('gab,gbm->gam', stiff_blocks[:, slot_index].astype(jnp.float32), picked, precision=highest_accuracy)
    return row_totals.reshape(number * BS, ADJUSTED_MODES).astype(jnp.bfloat16)

def blade_projections(mode_panel, stiff_image, row_blade):
    left_rows = mode_panel.astype(jnp.float32)
    right_rows = stiff_image.astype(jnp.float32)
    results = []
    for blade_index in range(NBLADE):
        masked = jnp.where((row_blade == blade_index)[:, None], left_rows, jnp.zeros_like(left_rows))
        results.append(jnp.dot(masked.T.astype(jnp.float32), right_rows.astype(jnp.float32), precision=highest_accuracy, preferred_element_type=jnp.float32))
    return jnp.stack(results)

def inverse_factor(inner_product_matrix):
    factor = jnp.linalg.cholesky(inner_product_matrix)
    identity = jnp.broadcast_to(jnp.eye(inner_product_matrix.shape[-1], dtype=inner_product_matrix.dtype), inner_product_matrix.shape)
    return lax.linalg.triangular_solve(factor, identity, left_side=True, lower=True)

def orthonormal(present_image):
    inner_product_matrix = jnp.einsum('rfd,rfc->rdc', present_image, present_image, precision=highest_accuracy) / ADJUSTED_MODES
    inverse = inverse_factor(inner_product_matrix)
    return jnp.einsum('zis,zts->zit', present_image, inverse, precision=highest_accuracy)

def reference(mode_panel, stiff_blocks, stiff_cols, row_blade, adjusted_values, deviations, start_block):
    stiff_image = stiffness_image(mode_panel, stiff_blocks, stiff_cols)
    projected = blade_projections(mode_panel, stiff_image, row_blade)
    reduced = jnp.einsum('zb,bij->zij', deviations, projected, precision=highest_accuracy) + jnp.diag(adjusted_values)[None]
    current = jnp.broadcast_to(start_block[None], (deviations.shape[0], ADJUSTED_MODES, S))
    for iteration in range(STEPS):
        present_image = jnp.einsum('zij,zjs->zis', reduced, current, precision=highest_accuracy)
        current = orthonormal(present_image)
    return (projected, current)
```

```python
import jax
import jax.numpy as jnp
from jax import lax
from jax.experimental import pallas as pl
from jax.experimental.pallas import tpu as pltpu
from jax.sharding import Mesh
from jax.sharding import PartitionSpec as P

MODES = 512
S = 128
BS = 128
NBR = 5
NBLADE = 4
STEPS = 2
SHARD = 16
OWN = 64
HIGHEST = lax.Precision.HIGHEST
F32 = jnp.float32
BF16 = jnp.bfloat16

DOF = ("zh", "zl", "yl", "co")
REAL = ("yh", "xx")


def dof_index():
    return lax.axis_index(DOF)


def real_index():
    return lax.axis_index(REAL)


def in_vmem(x):
    return pltpu.with_memory_space_constraint(x, pltpu.VMEM)


def in_hbm(x):
    return pltpu.with_memory_space_constraint(x, pltpu.HBM)


def image_pair(stiff_ref, panel_ref, cols_ref, row_in_ref, row, shift):
    images = []
    for t in range(2):
        blocks = jnp.concatenate([stiff_ref[row_in_ref + t, n] for n in range(NBR)], axis=1)
        picked = jnp.concatenate(
            [panel_ref[cols_ref[n, row + t] - shift] for n in range(NBR)], axis=0
        )
        images.append(jnp.dot(blocks, picked, preferred_element_type=F32).astype(BF16))
    return jnp.concatenate(images, axis=0)


def project(left, image):
    return lax.dot_general(left, image, (((0,), (0,)), ((), ())), preferred_element_type=F32)


def inner_kernel(cols_ref, stiff_hbm, panel_hbm, halves_ref, panel_ref, stiff_ref, panel_sem, stiff_sem):
    lanes = pl.ds(pl.multiple_of(real_index() // 2 * 128, 128), 128)
    first = dof_index() * SHARD
    panel_copies = [
        pltpu.make_async_copy(
            panel_hbm.at[4 * i : 4 * i + 4], panel_ref.at[4 * i : 4 * i + 4], panel_sem.at[i]
        )
        for i in range(4)
    ]
    stiff_copies = {
        q: pltpu.make_async_copy(
            stiff_hbm.at[2 * q : 2 * q + 2], stiff_ref.at[2 * q : 2 * q + 2], stiff_sem.at[q]
        )
        for q in (1, 2, 3, 4, 5, 6, 0, 7)
    }
    for copy in panel_copies:
        copy.start()
    for copy in stiff_copies.values():
        copy.start()
    for copy in panel_copies:
        copy.wait()
    for half in range(2):
        total = None
        for q in range(1 + 3 * half, 4 + 3 * half):
            stiff_copies[q].wait()
            row = 2 * q
            image = image_pair(stiff_ref, panel_ref, cols_ref, row, row, first)
            part = project(columns_pair(panel_ref, row, lanes), image)
            total = part if total is None else total + part
        halves_ref[half] = total
    stiff_copies[0].wait()
    stiff_copies[7].wait()


def columns_pair(panel_ref, row, lanes):
    return jnp.concatenate([panel_ref[row, :, lanes], panel_ref[row + 1, :, lanes]], axis=0)


def inner_rows(cols, stiff, panel):
    vmem = pl.BlockSpec(memory_space=pltpu.VMEM)
    hbm = pl.BlockSpec(memory_space=pltpu.HBM)
    return pl.pallas_call(
        inner_kernel,
        in_specs=[pl.BlockSpec(memory_space=pltpu.SMEM), hbm, hbm],
        out_specs=(vmem, vmem, vmem),
        out_shape=(
            pltpu.VMEM((2, BS, MODES), F32),
            pltpu.VMEM((SHARD, BS, MODES), BF16),
            pltpu.VMEM((SHARD, NBR, BS, BS), BF16),
        ),
        scratch_shapes=[pltpu.SemaphoreType.DMA((4,)), pltpu.SemaphoreType.DMA((8,))],
        name="inner_rows",
        compiler_params=pltpu.CompilerParams(vmem_limit_bytes=24 << 20),
    )(cols, in_hbm(stiff), in_hbm(panel))


def edge_kernel(cols_ref, stiff_ref, panel_ref, low, high, halves, out_ref, near, total):
    lanes = pl.ds(pl.multiple_of(real_index() // 2 * 128, 128), 128)
    dof = dof_index()
    last = dof % 16 == 15
    near[0, 0:2] = low[...]
    near[0, 2:6] = panel_ref[0:4]
    near[1, 0:4] = panel_ref[12:16]
    near[1, 4:6] = high[...]
    totals = []
    for side, (row, shift) in enumerate(((0, -2), (14, 12))):
        image = image_pair(stiff_ref, near.at[side], cols_ref, row, row, shift + dof * SHARD)
        totals.append(halves[side] + project(columns_pair(panel_ref, row, lanes), image))
    zero = jnp.zeros_like(totals[1])
    total[0] = totals[0] + jnp.where(last, zero, totals[1])
    total[1] = jnp.where(last, totals[1], zero)
    start = pl.multiple_of(real_index() % 2 * OWN, OWN)
    for j in range(SHARD):
        a, h = j // 2, j % 2
        for kind in range(2):
            out_ref[j, kind] = total[
                kind, pl.ds(pl.multiple_of(start + 8 * a, 8), 8), 256 * h : 256 * (h + 1)
            ]


def edge_rows(cols, stiff, panel, low, high, halves):
    vmem = pl.BlockSpec(memory_space=pltpu.VMEM)
    return pl.pallas_call(
        edge_kernel,
        in_specs=[pl.BlockSpec(memory_space=pltpu.SMEM)] + [vmem] * 5,
        out_specs=vmem,
        out_shape=jax.ShapeDtypeStruct((SHARD, 2, 8, 256), F32),
        scratch_shapes=[pltpu.VMEM((2, 6, BS, MODES), BF16), pltpu.VMEM((2, BS, MODES), F32)],
        name="edge_rows",
        compiler_params=pltpu.CompilerParams(vmem_limit_bytes=24 << 20),
    )(cols, *(in_vmem(x) for x in (stiff, panel, low, high, halves)))


def first_payload(pieces, label, start_row):
    total = jnp.sum(pieces, axis=0).reshape(16, 256)
    extra = jnp.concatenate([jnp.full((1, 256), label, F32), jnp.tile(start_row, 2)[None]], axis=0)
    return jnp.concatenate([total, jnp.pad(extra, ((0, 6), (0, 0)))], axis=0)


def second_payload(got):
    blocks = (got[:, 0:8] + jnp.roll(got[:, 8:16], 1, axis=0)).astype(BF16).reshape(32, 256)
    rows = got[:, 17, 0:S]
    high = rows.astype(BF16)
    rest = (rows - high.astype(F32)).astype(BF16)
    labels = got[:, 16, 0].astype(jnp.int32)
    rows = jnp.pad(jnp.concatenate([high, rest], axis=1), ((0, 4), (0, 0)))
    return jnp.concatenate([blocks, rows], axis=0), labels


def both(f, *lists):
    return [f(*items) for items in zip(*lists)]


def block_factor(cols, sub):
    a = [[jnp.broadcast_to(cols[j][i : i + 1, :], (8, S)) if i >= j else None for j in range(8)] for i in range(8)]
    roots = []
    low = [[None] * 8 for _ in range(8)]
    for t in range(8):
        roots.append(lax.rsqrt(a[t][t]))
        inverse = roots[t] * roots[t]
        for i in range(t + 1, 8):
            low[i][t] = a[i][t] * inverse
        for i in range(t + 1, 8):
            for j in range(t + 1, i + 1):
                a[i][j] = a[i][j] - low[i][t] * a[j][t]
    w = [[None] * 8 for _ in range(8)]
    for i in range(8):
        for j in range(i):
            total = low[i][j]
            for k in range(j + 1, i):
                total = total + low[i][k] * w[k][j]
            w[i][j] = -total
    scaled = [[w[i][j] * roots[i] if j < i else roots[i] for j in range(i + 1)] for i in range(8)]
    return scaled


def column_of(scaled, j, sub):
    out = jnp.zeros((8, S), F32)
    for i in range(j, 8):
        out = jnp.where(sub == i, scaled[i][j], out)
    return out


def twice(x):
    return jnp.concatenate([x, x], axis=1)


def apply_block(scaled, tile, sub):
    total = None
    for j in range(8):
        term = twice(column_of(scaled, j, sub)) * jnp.broadcast_to(tile[j : j + 1, :], (8, 2 * S))
        total = term if total is None else total + term
    return total


def lane_copy(tile, at):
    return jnp.broadcast_to(tile[:, at : at + 1], (8, S))


def gram_of(panel):
    high, low = split(panel)
    left_high, left_low = high[:, 0:S], low[:, 0:S]
    tall = dot(
        jnp.concatenate([left_high, left_low, left_high], axis=0),
        jnp.concatenate([high, high, low], axis=0),
        ((0,), (0,)),
    )
    return tall


def eliminate(work, sub):
    for p in range(S // 16):
        lo = 16 * p
        zs = range(2)
        one = [work[z, lo : lo + 8, :] for z in zs]
        two = [work[z, lo + 8 : lo + 16, :] for z in zs]
        cols = [[lane_copy(one[z], lo + j) for j in range(8)] for z in zs]
        cross = [[lane_copy(two[z], lo + j) for j in range(8)] for z in zs]
        scaled = [block_factor(cols[z], sub) for z in zs]
        one = [apply_block(scaled[z], one[z], sub) for z in zs]
        for i in range(8):
            for z in zs:
                ratio = None
                for j in range(i + 1):
                    term = cross[z][j] * scaled[z][i][j]
                    ratio = term if ratio is None else ratio + term
                two[z] = two[z] - twice(ratio) * jnp.broadcast_to(one[z][i : i + 1, :], (8, 2 * S))
        cols = [[lane_copy(two[z], lo + 8 + j) for j in range(8)] for z in zs]
        scaled = [block_factor(cols[z], sub) for z in zs]
        two = [apply_block(scaled[z], two[z], sub) for z in zs]
        panels = [jnp.concatenate([one[z], two[z]], axis=0) for z in zs]
        for z in zs:
            work[z, lo : lo + 16, :] = panels[z]
        if p < S // 16 - 1:
            change = [gram_of(panels[z]) for z in zs]
            for z in zs:
                work[z, lo + 16 :, :] -= change[z][lo + 16 :, :]


def split(x):
    high = x.astype(BF16)
    return high, (x - high.astype(F32)).astype(BF16)


def dot(a, b, dims=((1,), (0,))):
    return lax.dot_general(a, b, (dims, ((), ())), preferred_element_type=F32)


def product(high, low, right):
    right_high, right_low = split(right)
    wide = dot(high, jnp.concatenate([right_high, right_low], axis=1))
    return wide[:, 0:S] + wide[:, S:] + dot(low, right_high)


def solve_kernel(
    labels_ref, dev_ref, mine, other, values, proj_ref, out_ref,
    high_ref, low_ref, start_ref, image_ref, work,
):
    core = dof_index() % 2
    yh = real_index() // 4
    xx = real_index() % 4
    scale = [[dev_ref[z, labels_ref[k]] for k in range(NBLADE)] for z in range(2)]
    hit = lax.broadcasted_iota(jnp.int32, (8, 256), 1) - lax.broadcasted_iota(jnp.int32, (8, 256), 0)
    for parts, h in ((mine, core), (other, 1 - core)):

        def piece(src, y, k):
            return parts[src, y, 8 * k : 8 * k + 8, :].astype(F32)

        lanes = pl.ds(pl.multiple_of(256 * h, 256), 256)
        diagonal = jnp.broadcast_to(values[:, lanes], (8, 256))
        for zl in range(2):
            for x in range(4):
                src = zl * 4 + x
                for y in range(2):
                    for yl in range(4):
                        row = y * 256 + x * 64 + zl * 32 + yl * 8
                        blades = [piece(src, y * 4 + yl, k) for k in range(NBLADE)]
                        diag = jnp.where(hit == row - 256 * h, diagonal, 0.0)
                        for z in range(2):
                            tile = diag
                            for k in range(NBLADE):
                                tile += scale[z][k] * blades[k]
                            high, low = split(tile)
                            high_ref[z, row : row + 8, lanes] = high
                            low_ref[z, row : row + 8, lanes] = low
                        pair = parts[src, y * 4 + yl, 32:36, :].astype(F32)
                        top = y * 256 + x * 64 + zl * 16 + yl * 4
                        start_ref[pl.ds(pl.multiple_of(top + 32 * h, 4), 4), :] = pair[:, 0:S] + pair[:, S:]
            for yl in range(4):
                for k in range(NBLADE):
                    proj_ref[labels_ref[k], zl * 32 + yl * 8 : zl * 32 + yl * 8 + 8, lanes] = (
                        piece(zl * 4 + xx, yh * 4 + yl, k)
                    )

    eye = (
        lax.broadcasted_iota(jnp.int32, (S, S), 0) == lax.broadcasted_iota(jnp.int32, (S, S), 1)
    ).astype(F32)
    sub = lax.broadcasted_iota(jnp.int32, (8, S), 0)
    own = pl.ds(pl.multiple_of((yh * 4 + xx) * OWN, OWN), OWN)
    current = [start_ref[...]] * 2
    for step in range(STEPS):
        for z in range(2):
            image = product(high_ref[z], low_ref[z], current[z])
            image_ref[z] = image
            high, low = split(image)
            wide = dot(high, jnp.concatenate([high, low], axis=1), ((0,), (0,)))
            gram = wide[:, 0:S] + wide[:, S:] + dot(low, jnp.concatenate([high, low], axis=1), ((0,), (0,)))[:, 0:S]
            work[z, :, 0:S] = gram / MODES
            work[z, :, S : 2 * S] = eye
        eliminate(work, sub)
        if step < STEPS - 1:
            images = [image_ref[z] for z in range(2)]
        else:
            images = [image_ref[z, own, :] for z in range(2)]
        for z in range(2):
            high, low = split(images[z])
            inverse_high, inverse_low = split(work[z, :, S : 2 * S])
            wide = dot(high, jnp.concatenate([inverse_high, inverse_low], axis=0), ((1,), (1,)))
            current[z] = wide[:, 0:S] + wide[:, S:] + dot(low, inverse_high, ((1,), (1,)))
    for z in range(2):
        out_ref[z] = current[z]


def solve(labels, deviations, mine, other, values):
    smem = pl.BlockSpec(memory_space=pltpu.SMEM)
    vmem = pl.BlockSpec(memory_space=pltpu.VMEM)
    return pl.pallas_call(
        solve_kernel,
        in_specs=[smem, smem] + [vmem] * 3,
        out_specs=(vmem, vmem),
        out_shape=(
            jax.ShapeDtypeStruct((NBLADE, OWN, MODES), F32),
            jax.ShapeDtypeStruct((2, OWN, S), F32),
        ),
        scratch_shapes=[
            pltpu.VMEM((2, MODES, MODES), BF16),
            pltpu.VMEM((2, MODES, MODES), BF16),
            pltpu.VMEM((MODES, S), F32),
            pltpu.VMEM((2, MODES, S), F32),
            pltpu.VMEM((2, S, 2 * S), F32),
        ],
        name="solve",
        compiler_params=pltpu.CompilerParams(vmem_limit_bytes=24 << 20),
    )(labels, deviations, in_vmem(mine), in_vmem(other), values)


def spread(x, axes, count):
    return lax.all_to_all(jnp.broadcast_to(x[None], (count,) + x.shape), axes, 0, 0)


def on_device(mode_panel, stiff_blocks, stiff_cols, row_blade, adjusted_values, deviations, start_block):
    panel = mode_panel.reshape(SHARD, BS, MODES)
    count = 64
    low = lax.ppermute(panel[SHARD - 2 :], DOF, [(i, i + 1) for i in range(count - 1)])
    high = lax.ppermute(panel[:2], DOF, [(i + 1, i) for i in range(count - 1)])
    cols = stiff_cols.T
    halves, near_panel, near_stiff = inner_rows(cols, stiff_blocks, panel)
    pieces = edge_rows(cols, near_stiff, near_panel, low, high, halves)
    pieces = lax.all_to_all(pieces, ("zl", "yl", "co"), 0, 0)
    core = lax.axis_index("co")
    zl = lax.axis_index("zl")
    row = core * 32 + zl * 16 + lax.axis_index("yl") * 4 + lax.axis_index("zh")
    start_row = lax.dynamic_slice(start_block, (row, 0), (1, S))[0]
    payload = first_payload(pieces, row_blade[0].astype(F32), start_row)
    payload, labels = second_payload(spread(payload, ("zh",), 4))
    mine = spread(spread(payload, ("yh", "yl"), 8), ("zl", "xx"), 8)
    other = lax.ppermute(mine, "co", [(0, 1), (1, 0)])
    return solve(labels, deviations, mine, other, adjusted_values[None])


def solution(mesh):
    fine = Mesh(mesh.devices.reshape(4, 2, 4, 2, 2, 4), DOF + REAL)
    in_specs = (
        P(DOF, None),
        P(DOF, None, None, None),
        P(DOF, None),
        P(DOF),
        P(),
        P(DOF, None),
        P(REAL, None),
    )
    out_specs = (P(None, REAL, None), P(DOF, REAL, None))
    return jax.shard_map(on_device, mesh=fine, in_specs=in_specs, out_specs=out_specs, check_vma=False)
```

```python
import jax
import jax.numpy as jnp
from jax import lax
from jax.experimental import pallas as pl
from jax.experimental.pallas import tpu as pltpu
from jax.sharding import Mesh
from jax.sharding import PartitionSpec as P

MODES = 512
S = 128
BS = 128
NBR = 5
NBLADE = 4
STEPS = 2
SHARD = 16
OWN = 64
HIGHEST = lax.Precision.HIGHEST
F32 = jnp.float32
BF16 = jnp.bfloat16

DOF = ("zh", "zl", "yl", "co")
REAL = ("yh", "xx")


def dof_index():
    return lax.axis_index(DOF)


def real_index():
    return lax.axis_index(REAL)


def in_vmem(x):
    return pltpu.with_memory_space_constraint(x, pltpu.VMEM)


def in_hbm(x):
    return pltpu.with_memory_space_constraint(x, pltpu.HBM)


def image_pair(stiff_ref, panel_ref, cols_ref, row_in_ref, row, shift):
    images = []
    for t in range(2):
        blocks = jnp.concatenate([stiff_ref[row_in_ref + t, n] for n in range(NBR)], axis=1)
        picked = jnp.concatenate(
            [panel_ref[cols_ref[n, row + t] - shift] for n in range(NBR)], axis=0
        )
        images.append(jnp.dot(blocks, picked, preferred_element_type=F32).astype(BF16))
    return jnp.concatenate(images, axis=0)


def project(left, image):
    return lax.dot_general(left, image, (((0,), (0,)), ((), ())), preferred_element_type=F32)


def inner_kernel(cols_ref, stiff_hbm, panel_hbm, halves_ref, panel_ref, stiff_ref, panel_sem, stiff_sem):
    lanes = pl.ds(pl.multiple_of(real_index() // 2 * 128, 128), 128)
    first = dof_index() * SHARD
    panel_copies = [
        pltpu.make_async_copy(
            panel_hbm.at[4 * i : 4 * i + 4], panel_ref.at[4 * i : 4 * i + 4], panel_sem.at[i]
        )
        for i in range(4)
    ]
    stiff_copies = {
        q: pltpu.make_async_copy(
            stiff_hbm.at[2 * q : 2 * q + 2], stiff_ref.at[2 * q : 2 * q + 2], stiff_sem.at[q]
        )
        for q in (1, 2, 3, 4, 5, 6, 0, 7)
    }
    for copy in panel_copies:
        copy.start()
    for copy in stiff_copies.values():
        copy.start()
    for copy in panel_copies:
        copy.wait()
    for half in range(2):
        total = None
        for q in range(1 + 3 * half, 4 + 3 * half):
            stiff_copies[q].wait()
            row = 2 * q
            image = image_pair(stiff_ref, panel_ref, cols_ref, row, row, first)
            part = project(columns_pair(panel_ref, row, lanes), image)
            total = part if total is None else total + part
        halves_ref[half] = total
    stiff_copies[0].wait()
    stiff_copies[7].wait()


def columns_pair(panel_ref, row, lanes):
    return jnp.concatenate([panel_ref[row, :, lanes], panel_ref[row + 1, :, lanes]], axis=0)


def inner_rows(cols, stiff, panel):
    vmem = pl.BlockSpec(memory_space=pltpu.VMEM)
    hbm = pl.BlockSpec(memory_space=pltpu.HBM)
    return pl.pallas_call(
        inner_kernel,
        in_specs=[pl.BlockSpec(memory_space=pltpu.SMEM), hbm, hbm],
        out_specs=(vmem, vmem, vmem),
        out_shape=(
            pltpu.VMEM((2, BS, MODES), F32),
            pltpu.VMEM((SHARD, BS, MODES), BF16),
            pltpu.VMEM((SHARD, NBR, BS, BS), BF16),
        ),
        scratch_shapes=[pltpu.SemaphoreType.DMA((4,)), pltpu.SemaphoreType.DMA((8,))],
        name="inner_rows",
        compiler_params=pltpu.CompilerParams(vmem_limit_bytes=24 << 20),
    )(cols, in_hbm(stiff), in_hbm(panel))


def edge_kernel(cols_ref, stiff_ref, panel_ref, low, high, halves, out_ref, near, total):
    lanes = pl.ds(pl.multiple_of(real_index() // 2 * 128, 128), 128)
    dof = dof_index()
    last = dof % 16 == 15
    near[0, 0:2] = low[...]
    near[0, 2:6] = panel_ref[0:4]
    near[1, 0:4] = panel_ref[12:16]
    near[1, 4:6] = high[...]
    totals = []
    for side, (row, shift) in enumerate(((0, -2), (14, 12))):
        image = image_pair(stiff_ref, near.at[side], cols_ref, row, row, shift + dof * SHARD)
        totals.append(halves[side] + project(columns_pair(panel_ref, row, lanes), image))
    zero = jnp.zeros_like(totals[1])
    total[0] = totals[0] + jnp.where(last, zero, totals[1])
    total[1] = jnp.where(last, totals[1], zero)
    start = pl.multiple_of(real_index() % 2 * OWN, OWN)
    for j in range(SHARD):
        a, h = j // 2, j % 2
        for kind in range(2):
            out_ref[j, kind] = total[
                kind, pl.ds(pl.multiple_of(start + 8 * a, 8), 8), 256 * h : 256 * (h + 1)
            ]


def edge_rows(cols, stiff, panel, low, high, halves):
    vmem = pl.BlockSpec(memory_space=pltpu.VMEM)
    return pl.pallas_call(
        edge_kernel,
        in_specs=[pl.BlockSpec(memory_space=pltpu.SMEM)] + [vmem] * 5,
        out_specs=vmem,
        out_shape=jax.ShapeDtypeStruct((SHARD, 2, 8, 256), F32),
        scratch_shapes=[pltpu.VMEM((2, 6, BS, MODES), BF16), pltpu.VMEM((2, BS, MODES), F32)],
        name="edge_rows",
        compiler_params=pltpu.CompilerParams(vmem_limit_bytes=24 << 20),
    )(cols, *(in_vmem(x) for x in (stiff, panel, low, high, halves)))


def first_payload(pieces, label, start_row):
    total = jnp.sum(pieces, axis=0).reshape(16, 256)
    extra = jnp.concatenate([jnp.full((1, 256), label, F32), jnp.tile(start_row, 2)[None]], axis=0)
    return jnp.concatenate([total, jnp.pad(extra, ((0, 6), (0, 0)))], axis=0)


def second_payload(got):
    blocks = (got[:, 0:8] + jnp.roll(got[:, 8:16], 1, axis=0)).astype(BF16).reshape(32, 256)
    rows = got[:, 17, 0:S]
    high = rows.astype(BF16)
    rest = (rows - high.astype(F32)).astype(BF16)
    labels = got[:, 16, 0].astype(jnp.int32)
    rows = jnp.pad(jnp.concatenate([high, rest], axis=1), ((0, 4), (0, 0)))
    return jnp.concatenate([blocks, rows], axis=0), labels


def both(f, *lists):
    return [f(*items) for items in zip(*lists)]


def block_factor(cols, sub):
    a = [[jnp.broadcast_to(cols[j][i : i + 1, :], (8, S)) if i >= j else None for j in range(8)] for i in range(8)]
    roots = []
    low = [[None] * 8 for _ in range(8)]
    for t in range(8):
        roots.append(lax.rsqrt(a[t][t]))
        inverse = roots[t] * roots[t]
        for i in range(t + 1, 8):
            low[i][t] = a[i][t] * inverse
        for i in range(t + 1, 8):
            for j in range(t + 1, i + 1):
                a[i][j] = a[i][j] - low[i][t] * a[j][t]
    w = [[None] * 8 for _ in range(8)]
    for i in range(8):
        for j in range(i):
            total = low[i][j]
            for k in range(j + 1, i):
                total = total + low[i][k] * w[k][j]
            w[i][j] = -total
    scaled = [[w[i][j] * roots[i] if j < i else roots[i] for j in range(i + 1)] for i in range(8)]
    return scaled


def column_of(scaled, j, sub):
    out = jnp.zeros((8, S), F32)
    for i in range(j, 8):
        out = jnp.where(sub == i, scaled[i][j], out)
    return out


def twice(x):
    return jnp.concatenate([x, x], axis=1)


def apply_block(scaled, tile, sub):
    total = None
    for j in range(8):
        term = twice(column_of(scaled, j, sub)) * jnp.broadcast_to(tile[j : j + 1, :], (8, 2 * S))
        total = term if total is None else total + term
    return total


def lane_copy(tile, at):
    return jnp.broadcast_to(tile[:, at : at + 1], (8, S))


def gram_of(panel):
    high, low = split(panel)
    left_high, left_low = high[:, 0:S], low[:, 0:S]
    tall = dot(
        jnp.concatenate([left_high, left_low, left_high], axis=0),
        jnp.concatenate([high, high, low], axis=0),
        ((0,), (0,)),
    )
    return tall


def eliminate(work, sub):
    for p in range(S // 16):
        lo = 16 * p
        zs = range(2)
        one = [work[z, lo : lo + 8, :] for z in zs]
        two = [work[z, lo + 8 : lo + 16, :] for z in zs]
        cols = [[lane_copy(one[z], lo + j) for j in range(8)] for z in zs]
        cross = [[lane_copy(two[z], lo + j) for j in range(8)] for z in zs]
        scaled = [block_factor(cols[z], sub) for z in zs]
        one = [apply_block(scaled[z], one[z], sub) for z in zs]
        for i in range(8):
            for z in zs:
                ratio = None
                for j in range(i + 1):
                    term = cross[z][j] * scaled[z][i][j]
                    ratio = term if ratio is None else ratio + term
                two[z] = two[z] - twice(ratio) * jnp.broadcast_to(one[z][i : i + 1, :], (8, 2 * S))
        cols = [[lane_copy(two[z], lo + 8 + j) for j in range(8)] for z in zs]
        scaled = [block_factor(cols[z], sub) for z in zs]
        two = [apply_block(scaled[z], two[z], sub) for z in zs]
        panels = [jnp.concatenate([one[z], two[z]], axis=0) for z in zs]
        for z in zs:
            work[z, lo : lo + 16, :] = panels[z]
        if p < S // 16 - 1:
            change = [gram_of(panels[z]) for z in zs]
            for z in zs:
                work[z, lo + 16 :, :] -= change[z][lo + 16 :, :]


def split(x):
    high = x.astype(BF16)
    return high, (x - high.astype(F32)).astype(BF16)


def dot(a, b, dims=((1,), (0,))):
    return lax.dot_general(a, b, (dims, ((), ())), preferred_element_type=F32)


def product(halves, right_ref, z):
    total = None
    for high_ref, low_ref, first in halves:
        right_high, right_low = split(right_ref[pl.ds(pl.multiple_of(first, 256), 256), :])
        wide = dot(high_ref[z], jnp.concatenate([right_high, right_low], axis=1))
        part = wide[:, 0:S] + wide[:, S:] + dot(low_ref[z], right_high)
        total = part if total is None else total + part
    return total


def build(labels_ref, dev_ref, parts, values, h, high_ref, low_ref, start_ref, proj_ref):
    yh = real_index() // 4
    xx = real_index() % 4
    scale = [[dev_ref[z, labels_ref[k]] for k in range(NBLADE)] for z in range(2)]
    hit = lax.broadcasted_iota(jnp.int32, (8, 256), 1) - lax.broadcasted_iota(jnp.int32, (8, 256), 0)
    lanes = pl.ds(pl.multiple_of(256 * h, 256), 256)
    diagonal = jnp.broadcast_to(values[:, lanes], (8, 256))

    def piece(src, y, k):
        return parts[src, pl.ds(pl.multiple_of(32 * y + 8 * k, 8), 8), :].astype(F32)

    for zl in range(2):
        for x in range(4):
            src = zl * 4 + x
            for y in range(2):
                for yl in range(4):
                    row = y * 256 + x * 64 + zl * 32 + yl * 8
                    blades = [piece(src, y * 4 + yl, k) for k in range(NBLADE)]
                    diag = jnp.where(hit == row - 256 * h, diagonal, 0.0)
                    for z in range(2):
                        tile = diag
                        for k in range(NBLADE):
                            tile += scale[z][k] * blades[k]
                        high, low = split(tile)
                        high_ref[z, row : row + 8, :] = high
                        low_ref[z, row : row + 8, :] = low
                top = y * 128 + x * 32 + zl * 16
                pair = parts[src, 256 + 16 * y : 272 + 16 * y, :].astype(F32)
                start_ref[top : top + 16, :] = pair[:, 0:S] + pair[:, S:]
        for yl in range(4):
            for k in range(NBLADE):
                at = zl * 32 + yl * 8
                proj_ref[labels_ref[k], at : at + 8, :] = piece(zl * 4 + xx, yh * 4 + yl, k)


def prepare_kernel(labels_ref, dev_ref, mine, values, *outs):
    build(labels_ref, dev_ref, mine, values, dof_index() % 2, *outs)


HALF = (
    pltpu.VMEM((2, MODES, 256), BF16),
    pltpu.VMEM((2, MODES, 256), BF16),
    pltpu.VMEM((256, S), F32),
    pltpu.VMEM((NBLADE, OWN, 256), F32),
)
SMEM_SPEC = pl.BlockSpec(memory_space=pltpu.SMEM)
VMEM_SPEC = pl.BlockSpec(memory_space=pltpu.VMEM)


def prepare(labels, deviations, mine, values):
    return pl.pallas_call(
        prepare_kernel,
        in_specs=[SMEM_SPEC] * 2 + [VMEM_SPEC] * 2,
        out_specs=(VMEM_SPEC,) * 4,
        out_shape=HALF,
        name="prepare",
        compiler_params=pltpu.CompilerParams(vmem_limit_bytes=24 << 20),
    )(labels, deviations, in_vmem(mine), values)


def solve_kernel(
    labels_ref, dev_ref, other, values, mine_high, mine_low, mine_start, mine_proj,
    proj_ref, out_ref, high_ref, low_ref, half_start, half_proj, start_ref, image_ref, work,
):
    core = dof_index() % 2
    build(labels_ref, dev_ref, other, values, 1 - core, high_ref, low_ref, half_start, half_proj)
    for start, proj, h in ((mine_start, mine_proj, core), (half_start, half_proj, 1 - core)):
        for block in range(8):
            rows = pl.ds(pl.multiple_of(64 * block + 32 * h, 32), 32)
            start_ref[rows, :] = start[32 * block : 32 * block + 32, :]
        proj_ref[:, :, pl.ds(pl.multiple_of(256 * h, 256), 256)] = proj[...]
    halves = ((mine_high, mine_low, 256 * core), (high_ref, low_ref, 256 * (1 - core)))

    eye = (
        lax.broadcasted_iota(jnp.int32, (S, S), 0) == lax.broadcasted_iota(jnp.int32, (S, S), 1)
    ).astype(F32)
    sub = lax.broadcasted_iota(jnp.int32, (8, S), 0)
    own = pl.ds(pl.multiple_of(real_index() * OWN, OWN), OWN)
    for step in range(STEPS):
        for z in range(2):
            image = product(halves, start_ref if step == 0 else image_ref.at[z], z)
            image_ref[z] = image
            high, low = split(image)
            wide = dot(high, jnp.concatenate([high, low], axis=1), ((0,), (0,)))
            work[z, :, 0:S] = (wide[:, 0:S] + wide[:, S:] + dot(low, high, ((0,), (0,)))) / MODES
            work[z, :, S : 2 * S] = eye
        eliminate(work, sub)
        for z in range(2):
            high, low = split(image_ref[z] if step < STEPS - 1 else image_ref[z, own, :])
            inverse_high, inverse_low = split(work[z, :, S : 2 * S])
            wide = dot(high, jnp.concatenate([inverse_high, inverse_low], axis=0), ((1,), (1,)))
            current = wide[:, 0:S] + wide[:, S:] + dot(low, inverse_high, ((1,), (1,)))
            if step < STEPS - 1:
                image_ref[z] = current
            else:
                out_ref[z] = current


def solve(labels, deviations, mine, other, values):
    ready = prepare(labels, deviations, mine, values)
    return pl.pallas_call(
        solve_kernel,
        in_specs=[SMEM_SPEC] * 2 + [VMEM_SPEC] * 6,
        out_specs=(VMEM_SPEC, VMEM_SPEC),
        out_shape=(
            jax.ShapeDtypeStruct((NBLADE, OWN, MODES), F32),
            jax.ShapeDtypeStruct((2, OWN, S), F32),
        ),
        scratch_shapes=[
            *HALF,
            pltpu.VMEM((MODES, S), F32),
            pltpu.VMEM((2, MODES, S), F32),
            pltpu.VMEM((2, S, 2 * S), F32),
        ],
        name="solve",
        compiler_params=pltpu.CompilerParams(vmem_limit_bytes=24 << 20),
    )(labels, deviations, in_vmem(other), values, *(in_vmem(x) for x in ready))


def spread(x, axes, count):
    return lax.all_to_all(jnp.broadcast_to(x[None], (count,) + x.shape), axes, 0, 0)


def on_device(mode_panel, stiff_blocks, stiff_cols, row_blade, adjusted_values, deviations, start_block):
    panel = mode_panel.reshape(SHARD, BS, MODES)
    count = 64
    low = lax.ppermute(panel[SHARD - 2 :], DOF, [(i, i + 1) for i in range(count - 1)])
    high = lax.ppermute(panel[:2], DOF, [(i + 1, i) for i in range(count - 1)])
    cols = stiff_cols.T
    halves, near_panel, near_stiff = inner_rows(cols, stiff_blocks, panel)
    pieces = edge_rows(cols, near_stiff, near_panel, low, high, halves)
    pieces = lax.all_to_all(pieces, ("zl", "yl", "co"), 0, 0)
    core = lax.axis_index("co")
    zl = lax.axis_index("zl")
    row = core * 32 + zl * 16 + lax.axis_index("yl") * 4 + lax.axis_index("zh")
    start_row = lax.dynamic_slice(start_block, (row, 0), (1, S))[0]
    payload = first_payload(pieces, row_blade[0].astype(F32), start_row)
    payload, labels = second_payload(spread(payload, ("zh",), 4))
    ring = spread(payload, ("yh", "yl"), 8)
    mine = jnp.concatenate([ring[:, 0:32].reshape(256, 256), ring[:, 32:36].reshape(32, 256)], axis=0)
    mine = spread(mine, ("zl", "xx"), 8)
    other = lax.ppermute(mine, "co", [(0, 1), (1, 0)])
    return solve(labels, deviations, mine, other, adjusted_values[None])


def solution(mesh):
    fine = Mesh(mesh.devices.reshape(4, 2, 4, 2, 2, 4), DOF + REAL)
    in_specs = (
        P(DOF, None),
        P(DOF, None, None, None),
        P(DOF, None),
        P(DOF),
        P(),
        P(DOF, None),
        P(REAL, None),
    )
    out_specs = (P(None, REAL, None), P(DOF, REAL, None))
    return jax.shard_map(on_device, mesh=fine, in_specs=in_specs, out_specs=out_specs, check_vma=False)
```

```python
import jax
import jax.numpy as jnp
from jax import lax
from jax.experimental import pallas as pl
from jax.experimental.pallas import tpu as pltpu
from jax.sharding import Mesh
from jax.sharding import PartitionSpec as P

MODES = 512
S = 128
BS = 128
NBR = 5
NBLADE = 4
STEPS = 2
SHARD = 16
OWN = 64
HIGHEST = lax.Precision.HIGHEST
F32 = jnp.float32
BF16 = jnp.bfloat16

DOF = ("zh", "zl", "yl", "co")
REAL = ("yh", "xx")


def dof_index():
    return lax.axis_index(DOF)


def real_index():
    return lax.axis_index(REAL)


def in_vmem(x):
    return pltpu.with_memory_space_constraint(x, pltpu.VMEM)


def in_hbm(x):
    return pltpu.with_memory_space_constraint(x, pltpu.HBM)


def image_pair(stiff_ref, panel_ref, cols_ref, row_in_ref, row, shift):
    images = []
    for t in range(2):
        blocks = jnp.concatenate([stiff_ref[row_in_ref + t, n] for n in range(NBR)], axis=1)
        picked = jnp.concatenate(
            [panel_ref[cols_ref[n, row + t] - shift] for n in range(NBR)], axis=0
        )
        images.append(jnp.dot(blocks, picked, preferred_element_type=F32).astype(BF16))
    return jnp.concatenate(images, axis=0)


def project(left, image):
    return lax.dot_general(left, image, (((0,), (0,)), ((), ())), preferred_element_type=F32)


def inner_kernel(cols_ref, stiff_hbm, panel_hbm, halves_ref, panel_ref, stiff_ref, panel_sem, stiff_sem):
    lanes = pl.ds(pl.multiple_of(real_index() // 2 * 128, 128), 128)
    first = dof_index() * SHARD
    panel_copies = [
        pltpu.make_async_copy(
            panel_hbm.at[4 * i : 4 * i + 4], panel_ref.at[4 * i : 4 * i + 4], panel_sem.at[i]
        )
        for i in range(4)
    ]
    stiff_copies = {
        q: pltpu.make_async_copy(
            stiff_hbm.at[2 * q : 2 * q + 2], stiff_ref.at[2 * q : 2 * q + 2], stiff_sem.at[q]
        )
        for q in (1, 2, 3, 4, 5, 6, 0, 7)
    }
    for copy in panel_copies:
        copy.start()
    for copy in stiff_copies.values():
        copy.start()
    for copy in panel_copies:
        copy.wait()
    for half in range(2):
        total = None
        for q in range(1 + 3 * half, 4 + 3 * half):
            stiff_copies[q].wait()
            row = 2 * q
            image = image_pair(stiff_ref, panel_ref, cols_ref, row, row, first)
            part = project(columns_pair(panel_ref, row, lanes), image)
            total = part if total is None else total + part
        halves_ref[half] = total
    stiff_copies[0].wait()
    stiff_copies[7].wait()


def columns_pair(panel_ref, row, lanes):
    return jnp.concatenate([panel_ref[row, :, lanes], panel_ref[row + 1, :, lanes]], axis=0)


def inner_rows(cols, stiff, panel):
    vmem = pl.BlockSpec(memory_space=pltpu.VMEM)
    hbm = pl.BlockSpec(memory_space=pltpu.HBM)
    return pl.pallas_call(
        inner_kernel,
        in_specs=[pl.BlockSpec(memory_space=pltpu.SMEM), hbm, hbm],
        out_specs=(vmem, vmem, vmem),
        out_shape=(
            pltpu.VMEM((2, BS, MODES), F32),
            pltpu.VMEM((SHARD, BS, MODES), BF16),
            pltpu.VMEM((SHARD, NBR, BS, BS), BF16),
        ),
        scratch_shapes=[pltpu.SemaphoreType.DMA((4,)), pltpu.SemaphoreType.DMA((8,))],
        name="inner_rows",
        compiler_params=pltpu.CompilerParams(vmem_limit_bytes=24 << 20),
    )(cols, in_hbm(stiff), in_hbm(panel))


def edge_kernel(cols_ref, stiff_ref, panel_ref, low, high, halves, out_ref, near, total):
    lanes = pl.ds(pl.multiple_of(real_index() // 2 * 128, 128), 128)
    dof = dof_index()
    last = dof % 16 == 15
    near[0, 0:2] = low[...]
    near[0, 2:6] = panel_ref[0:4]
    near[1, 0:4] = panel_ref[12:16]
    near[1, 4:6] = high[...]
    totals = []
    for side, (row, shift) in enumerate(((0, -2), (14, 12))):
        image = image_pair(stiff_ref, near.at[side], cols_ref, row, row, shift + dof * SHARD)
        totals.append(halves[side] + project(columns_pair(panel_ref, row, lanes), image))
    total[0] = jnp.where(last, totals[1], totals[0] + totals[1])
    total[1] = totals[0]
    start = pl.multiple_of(real_index() % 2 * OWN, OWN)
    for j in range(SHARD):
        a, h = j // 2, j % 2
        rows = pl.ds(pl.multiple_of(start + 8 * a, 8), 8)
        for kind in range(2):
            out_ref[kind, j] = total[kind, rows, 256 * h : 256 * (h + 1)]


def edge_rows(cols, stiff, panel, low, high, halves):
    vmem = pl.BlockSpec(memory_space=pltpu.VMEM)
    return pl.pallas_call(
        edge_kernel,
        in_specs=[pl.BlockSpec(memory_space=pltpu.SMEM)] + [vmem] * 5,
        out_specs=vmem,
        out_shape=jax.ShapeDtypeStruct((2, SHARD, 8, 256), F32),
        scratch_shapes=[pltpu.VMEM((2, 6, BS, MODES), BF16), pltpu.VMEM((2, BS, MODES), F32)],
        name="edge_rows",
        compiler_params=pltpu.CompilerParams(vmem_limit_bytes=24 << 20),
    )(cols, *(in_vmem(x) for x in (stiff, panel, low, high, halves)))


def first_payload(pieces, label, start_row):
    total = jnp.concatenate([jnp.sum(pieces[:15], axis=0), pieces[15]], axis=0)
    extra = jnp.concatenate([jnp.full((1, 256), label, F32), jnp.tile(start_row, 2)[None]], axis=0)
    return jnp.concatenate([total, jnp.pad(extra, ((0, 6), (0, 0)))], axis=0)


def second_payload(got):
    blocks = (got[:, 0:8] + jnp.roll(got[:, 8:16], 1, axis=0)).astype(BF16).reshape(32, 256)
    rows = got[:, 17, 0:S]
    high = rows.astype(BF16)
    rest = (rows - high.astype(F32)).astype(BF16)
    labels = got[:, 16, 0].astype(jnp.int32)
    rows = jnp.pad(jnp.concatenate([high, rest], axis=1), ((0, 4), (0, 0)))
    return jnp.concatenate([blocks, rows], axis=0), labels


def both(f, *lists):
    return [f(*items) for items in zip(*lists)]


def block_factor(cols, sub):
    a = [[jnp.broadcast_to(cols[j][i : i + 1, :], (8, S)) if i >= j else None for j in range(8)] for i in range(8)]
    roots = []
    low = [[None] * 8 for _ in range(8)]
    for t in range(8):
        roots.append(lax.rsqrt(a[t][t]))
        inverse = roots[t] * roots[t]
        for i in range(t + 1, 8):
            low[i][t] = a[i][t] * inverse
        for i in range(t + 1, 8):
            for j in range(t + 1, i + 1):
                a[i][j] = a[i][j] - low[i][t] * a[j][t]
    w = [[None] * 8 for _ in range(8)]
    for i in range(8):
        for j in range(i):
            total = low[i][j]
            for k in range(j + 1, i):
                total = total + low[i][k] * w[k][j]
            w[i][j] = -total
    scaled = [[w[i][j] * roots[i] if j < i else roots[i] for j in range(i + 1)] for i in range(8)]
    return scaled


def column_of(scaled, j, sub):
    out = jnp.zeros((8, S), F32)
    for i in range(j, 8):
        out = jnp.where(sub == i, scaled[i][j], out)
    return out


def twice(x):
    return jnp.concatenate([x, x], axis=1)


def apply_block(scaled, tile, sub):
    total = None
    for j in range(8):
        term = twice(column_of(scaled, j, sub)) * jnp.broadcast_to(tile[j : j + 1, :], (8, 2 * S))
        total = term if total is None else total + term
    return total


def lane_copy(tile, at):
    return jnp.broadcast_to(tile[:, at : at + 1], (8, S))


def gram_of(panel):
    high, low = split(panel)
    left_high, left_low = high[:, 0:S], low[:, 0:S]
    tall = dot(
        jnp.concatenate([left_high, left_low, left_high], axis=0),
        jnp.concatenate([high, high, low], axis=0),
        ((0,), (0,)),
    )
    return tall


def eliminate(work, sub):
    for p in range(S // 16):
        lo = 16 * p
        zs = range(2)
        one = [work[z, lo : lo + 8, :] for z in zs]
        two = [work[z, lo + 8 : lo + 16, :] for z in zs]
        cols = [[lane_copy(one[z], lo + j) for j in range(8)] for z in zs]
        cross = [[lane_copy(two[z], lo + j) for j in range(8)] for z in zs]
        scaled = [block_factor(cols[z], sub) for z in zs]
        one = [apply_block(scaled[z], one[z], sub) for z in zs]
        for i in range(8):
            for z in zs:
                ratio = None
                for j in range(i + 1):
                    term = cross[z][j] * scaled[z][i][j]
                    ratio = term if ratio is None else ratio + term
                two[z] = two[z] - twice(ratio) * jnp.broadcast_to(one[z][i : i + 1, :], (8, 2 * S))
        cols = [[lane_copy(two[z], lo + 8 + j) for j in range(8)] for z in zs]
        scaled = [block_factor(cols[z], sub) for z in zs]
        two = [apply_block(scaled[z], two[z], sub) for z in zs]
        panels = [jnp.concatenate([one[z], two[z]], axis=0) for z in zs]
        for z in zs:
            work[z, lo : lo + 16, :] = panels[z]
        if p < S // 16 - 1:
            change = [gram_of(panels[z]) for z in zs]
            for z in zs:
                work[z, lo + 16 :, :] -= change[z][lo + 16 :, :]


def split(x):
    high = x.astype(BF16)
    return high, (x - high.astype(F32)).astype(BF16)


def dot(a, b, dims=((1,), (0,))):
    return lax.dot_general(a, b, (dims, ((), ())), preferred_element_type=F32)


def product(halves, right_ref, z):
    total = None
    for high_ref, low_ref, first in halves:
        right_high, right_low = split(right_ref[pl.ds(pl.multiple_of(first, 256), 256), :])
        wide = dot(high_ref[z], jnp.concatenate([right_high, right_low], axis=1))
        part = wide[:, 0:S] + wide[:, S:] + dot(low_ref[z], right_high)
        total = part if total is None else total + part
    return total


def build(labels_ref, dev_ref, parts, values, h, high_ref, low_ref, start_ref, proj_ref):
    yh = real_index() // 4
    xx = real_index() % 4
    scale = [[dev_ref[z, labels_ref[k]] for k in range(NBLADE)] for z in range(2)]
    hit = lax.broadcasted_iota(jnp.int32, (8, 256), 1) - lax.broadcasted_iota(jnp.int32, (8, 256), 0)
    lanes = pl.ds(pl.multiple_of(256 * h, 256), 256)
    diagonal = jnp.broadcast_to(values[:, lanes], (8, 256))

    def piece(src, y, k):
        return parts[src, pl.ds(pl.multiple_of(32 * y + 8 * k, 8), 8), :].astype(F32)

    for zl in range(2):
        for x in range(4):
            src = zl * 4 + x
            for y in range(2):
                for yl in range(4):
                    row = y * 256 + x * 64 + zl * 32 + yl * 8
                    blades = [piece(src, y * 4 + yl, k) for k in range(NBLADE)]
                    diag = jnp.where(hit == row - 256 * h, diagonal, 0.0)
                    for z in range(2):
                        tile = diag
                        for k in range(NBLADE):
                            tile += scale[z][k] * blades[k]
                        high, low = split(tile)
                        high_ref[z, row : row + 8, :] = high
                        low_ref[z, row : row + 8, :] = low
                top = y * 128 + x * 32 + zl * 16
                pair = parts[src, 256 + 16 * y : 272 + 16 * y, :].astype(F32)
                start_ref[top : top + 16, :] = pair[:, 0:S] + pair[:, S:]
        for yl in range(4):
            for k in range(NBLADE):
                at = zl * 32 + yl * 8
                proj_ref[labels_ref[k], at : at + 8, :] = piece(zl * 4 + xx, yh * 4 + yl, k)


def prepare_kernel(labels_ref, dev_ref, mine, values, *outs):
    build(labels_ref, dev_ref, mine, values, dof_index() % 2, *outs)


HALF = (
    pltpu.VMEM((2, MODES, 256), BF16),
    pltpu.VMEM((2, MODES, 256), BF16),
    pltpu.VMEM((256, S), F32),
    pltpu.VMEM((NBLADE, OWN, 256), F32),
)
SMEM_SPEC = pl.BlockSpec(memory_space=pltpu.SMEM)
VMEM_SPEC = pl.BlockSpec(memory_space=pltpu.VMEM)


def prepare(labels, deviations, mine, values):
    return pl.pallas_call(
        prepare_kernel,
        in_specs=[SMEM_SPEC] * 2 + [VMEM_SPEC] * 2,
        out_specs=(VMEM_SPEC,) * 4,
        out_shape=HALF,
        name="prepare",
        compiler_params=pltpu.CompilerParams(vmem_limit_bytes=24 << 20),
    )(labels, deviations, in_vmem(mine), values)


def solve_kernel(
    labels_ref, dev_ref, other, values, mine_high, mine_low, mine_start, mine_proj,
    proj_ref, out_ref, high_ref, low_ref, half_start, half_proj, start_ref, image_ref, work,
):
    core = dof_index() % 2
    build(labels_ref, dev_ref, other, values, 1 - core, high_ref, low_ref, half_start, half_proj)
    for start, proj, h in ((mine_start, mine_proj, core), (half_start, half_proj, 1 - core)):
        for block in range(8):
            rows = pl.ds(pl.multiple_of(64 * block + 32 * h, 32), 32)
            start_ref[rows, :] = start[32 * block : 32 * block + 32, :]
        proj_ref[:, :, pl.ds(pl.multiple_of(256 * h, 256), 256)] = proj[...]
    halves = ((mine_high, mine_low, 256 * core), (high_ref, low_ref, 256 * (1 - core)))

    eye = (
        lax.broadcasted_iota(jnp.int32, (S, S), 0) == lax.broadcasted_iota(jnp.int32, (S, S), 1)
    ).astype(F32)
    sub = lax.broadcasted_iota(jnp.int32, (8, S), 0)
    own = pl.ds(pl.multiple_of(real_index() * OWN, OWN), OWN)
    for step in range(STEPS):
        for z in range(2):
            image = product(halves, start_ref if step == 0 else image_ref.at[z], z)
            image_ref[z] = image
            high, low = split(image)
            wide = dot(high, jnp.concatenate([high, low], axis=1), ((0,), (0,)))
            work[z, :, 0:S] = (wide[:, 0:S] + wide[:, S:] + dot(low, high, ((0,), (0,)))) / MODES
            work[z, :, S : 2 * S] = eye
        eliminate(work, sub)
        for z in range(2):
            high, low = split(image_ref[z] if step < STEPS - 1 else image_ref[z, own, :])
            inverse_high, inverse_low = split(work[z, :, S : 2 * S])
            wide = dot(high, jnp.concatenate([inverse_high, inverse_low], axis=0), ((1,), (1,)))
            current = wide[:, 0:S] + wide[:, S:] + dot(low, inverse_high, ((1,), (1,)))
            if step < STEPS - 1:
                image_ref[z] = current
            else:
                out_ref[z] = current


def solve(labels, deviations, mine, other, values):
    ready = prepare(labels, deviations, mine, values)
    return pl.pallas_call(
        solve_kernel,
        in_specs=[SMEM_SPEC] * 2 + [VMEM_SPEC] * 6,
        out_specs=(VMEM_SPEC, VMEM_SPEC),
        out_shape=(
            jax.ShapeDtypeStruct((NBLADE, OWN, MODES), F32),
            jax.ShapeDtypeStruct((2, OWN, S), F32),
        ),
        scratch_shapes=[
            *HALF,
            pltpu.VMEM((MODES, S), F32),
            pltpu.VMEM((2, MODES, S), F32),
            pltpu.VMEM((2, S, 2 * S), F32),
        ],
        name="solve",
        compiler_params=pltpu.CompilerParams(vmem_limit_bytes=24 << 20),
    )(labels, deviations, in_vmem(other), values, *(in_vmem(x) for x in ready))


def spread(x, axes, count):
    return lax.all_to_all(jnp.broadcast_to(x[None], (count,) + x.shape), axes, 0, 0)


def on_device(mode_panel, stiff_blocks, stiff_cols, row_blade, adjusted_values, deviations, start_block):
    panel = mode_panel.reshape(SHARD, BS, MODES)
    count = 64
    low = lax.ppermute(panel[SHARD - 2 :], DOF, [(i, i + 1) for i in range(count - 1)])
    high = lax.ppermute(panel[:2], DOF, [(i + 1, i) for i in range(count - 1)])
    cols = stiff_cols.T
    halves, near_panel, near_stiff = inner_rows(cols, stiff_blocks, panel)
    pieces = edge_rows(cols, near_stiff, near_panel, low, high, halves)
    passed = lax.ppermute(pieces[1], DOF, [(16 * k + 15, 16 * k + 14) for k in range(4)])
    pieces = lax.all_to_all(pieces[0] + passed, ("zl", "yl", "co"), 0, 0)
    core = lax.axis_index("co")
    zl = lax.axis_index("zl")
    row = core * 32 + zl * 16 + lax.axis_index("yl") * 4 + lax.axis_index("zh")
    start_row = lax.dynamic_slice(start_block, (row, 0), (1, S))[0]
    payload = first_payload(pieces, row_blade[0].astype(F32), start_row)
    payload, labels = second_payload(spread(payload, ("zh",), 4))
    ring = spread(payload, ("yh", "yl"), 8)
    mine = jnp.concatenate([ring[:, 0:32].reshape(256, 256), ring[:, 32:36].reshape(32, 256)], axis=0)
    mine = spread(mine, ("zl", "xx"), 8)
    other = lax.ppermute(mine, "co", [(0, 1), (1, 0)])
    return solve(labels, deviations, mine, other, adjusted_values[None])


def solution(mesh):
    fine = Mesh(mesh.devices.reshape(4, 2, 4, 2, 2, 4), DOF + REAL)
    in_specs = (
        P(DOF, None),
        P(DOF, None, None, None),
        P(DOF, None),
        P(DOF),
        P(),
        P(DOF, None),
        P(REAL, None),
    )
    out_specs = (P(None, REAL, None), P(DOF, REAL, None))
    return jax.shard_map(on_device, mesh=fine, in_specs=in_specs, out_specs=out_specs, check_vma=False)
```
